128 devices in a mesh: obs: 8 (over x, y_lo), par: 16 (over z, y_hi, core).
Axes of the slice: x: 4, y: 4 (y_hi: 2, y_lo: 2; y = y_hi * 2 + y_lo), z: 4, core: 2. Of those that a mesh axis runs over, the one named last changes fastest.
Arguments:
- design: bfloat16 [1024, 24576], P('obs', 'par'), may hold values from -3 to 3
- filter_taps: float32 [2, 512], replicated, may hold values from -0.4 to 5
- band_limit: int32 [2], replicated, may hold values from 128 to 512, as said below
- col_order: int32 [16], replicated, may hold values from 0 to 15, each once
Outputs:
- normal: float32 [24576, 24576], P('par', 'obs')
The draws below stay inside these ranges and needn't reach their ends.
Inputs may be any that keep to these rules, and one draw needn't show every extreme that they name: col_order names every parameter block once. `band_limit`: the first arc batch uses all 512 lags.
All inputs are finite; a program needn't handle non-finite values.
Results may differ from the reference program's by a relative error of at most 0.0051.
Values may be sent and summed in bfloat16 or wider, within the bound.
No kernel may reach another device: no remote copies, remote signals or barrier semaphores. Data moves between devices by JAX's collectives and lax.ppermute only.
A program may use at most 128 MiB of HBM per device.

```python
import jax
import jax.numpy as jnp
from jax import lax

PAR_DEV = 1536
ARC_LEN = 512
ARCS = 2
OBS = 1024
PAR = 24576
N_PAR = 16


def draw_band_limit(key, part):
    rest = jax.random.randint(jax.random.fold_in(key, 17), (ARCS,), ARC_LEN // 4, ARC_LEN // 2 + 1)
    first = lax.broadcasted_iota(jnp.int32, (ARCS,), 0) == 0
    return jnp.where(first, jnp.full((ARCS,), ARC_LEN, jnp.int32), rest).astype(jnp.int32)


def draw_filter_taps(key, part):
    spread = 1.1 * (2.0 * ARC_LEN) ** (-0.5)
    rough_key = jax.random.fold_in(key, 31)
    lead_key = jax.random.fold_in(key, 37)
    rough = jax.random.normal(rough_key, (ARCS, ARC_LEN), jnp.float32) * spread
    lead = jax.random.uniform(lead_key, (ARCS, 1), jnp.float32, 3.5, 4.5)
    rough = jnp.clip(rough, -0.4, 0.4)
    first_lag = lax.broadcasted_iota(jnp.int32, (ARCS, ARC_LEN), 1) == 0
    return jnp.where(first_lag, jnp.broadcast_to(lead, (ARCS, ARC_LEN)), rough).astype(jnp.float32)


def steps_of(stream_key, dims, cuts, low, largest):
    level, own = 1.0, jax.random.fold_in(stream_key, 6)
    for position, shards_of in cuts:
        draws = jnp.exp(jax.random.uniform(jax.random.fold_in(own, position), (shards_of,), jnp.float32, low / len(cuts), largest / len(cuts)))
        level = level * jnp.repeat(draws, dims[position] // shards_of).reshape([-1 if axis == position else 1 for axis in range(len(dims))])
    return level


def normal_values(rng, dims, width, bound, pieces=(), kind=jnp.bfloat16):
    level = steps_of(rng, dims, pieces, -0.22, 0.18) if pieces else 1.0
    result = jax.random.normal(rng, dims, jnp.float32) * width * level
    return jnp.minimum(jnp.maximum(result, -bound), bound).astype(kind)


def setup_inputs(seed: int = 0) -> dict:
    arg_keys = jax.random.split(jax.random.key(seed), 5)
    return {
        "design": normal_values(arg_keys[0], (OBS, PAR), 0.5, 3.0, ((0, 8), (1, 16))),
        "filter_taps": draw_filter_taps(jax.random.fold_in(arg_keys[4], 71), 0),
        "band_limit": draw_band_limit(jax.random.fold_in(arg_keys[4], 71), 0),
        "col_order": jax.random.permutation(arg_keys[3], N_PAR).astype(jnp.int32),
    }


def arc_filters(filter_taps, band_limit):
    offsets = lax.broadcasted_iota(jnp.int32, (ARC_LEN, ARC_LEN), 0) - lax.broadcasted_iota(jnp.int32, (ARC_LEN, ARC_LEN), 1)
    distance = jnp.abs(offsets)

    def single(taps_row, limit_value):
        values = taps_row.astype(jnp.bfloat16)[distance]
        inside = distance < limit_value
        return jnp.where(inside, values, jnp.zeros_like(values))

    return jax.vmap(single)(filter_taps, band_limit)


def reference(design, filter_taps, band_limit, col_order):
    filters = arc_filters(filter_taps, band_limit)
    blocks = design.reshape(ARC_LEN, ARCS, PAR)
    filtered = jnp.einsum("ats,sap->tap", filters.astype(jnp.float32), blocks.astype(jnp.float32), precision=lax.Precision.HIGHEST)
    filtered = filtered.astype(jnp.bfloat16).reshape(OBS, PAR)
    widened = filtered.astype(jnp.float32)
    reordered = widened.reshape(OBS, N_PAR, PAR_DEV)[:, col_order, :].reshape(OBS, PAR)
    return jnp.dot(widened.T, reordered, precision=lax.Precision.HIGHEST) / OBS
```

```python
import jax
import jax.numpy as jnp
from jax import lax
from jax.experimental import pallas as pl
from jax.experimental.pallas import tpu as pltpu
from jax.sharding import Mesh
from jax.sharding import PartitionSpec as P


X, YL, Z, YH, C = 4, 2, 4, 2, 2
BF16 = jnp.bfloat16
F32 = jnp.float32


def shift(array, axis, size, step=1):
    return lax.ppermute(array, axis, [(i, (i + step) % size) for i in range(size)])


def sds(shape, dtype=BF16):
    return jax.ShapeDtypeStruct(shape, dtype)


def split_shard(design):
    rows, cols = design.shape
    half, width = rows // 2, cols // Z

    def kernel(d_ref, o_ref):
        r = lax.broadcasted_iota(jnp.int32, (rows, rows), 0)
        s = lax.broadcasted_iota(jnp.int32, (rows, rows), 1)
        source = jnp.where(r < half, 2 * r, 2 * (r - half) + 1)
        pick = (s == source).astype(F32).astype(BF16)
        sorted_rows = jnp.dot(pick, d_ref[...], preferred_element_type=F32).astype(BF16)
        for q in range(Z):
            for a in range(2):
                o_ref[q, a] = sorted_rows[a * half:(a + 1) * half, q * width:(q + 1) * width]

    return pl.pallas_call(kernel, out_shape=sds((Z, 2, half, width)), name="split_shard")(design)


def build_filters(taps, band):
    arcs, n = taps.shape

    def kernel(band_ref, taps_ref, o_ref):
        lag = lax.broadcasted_iota(jnp.int32, (n, 2 * n), 0)
        pos = lax.broadcasted_iota(jnp.int32, (n, 2 * n), 1)
        spread = (jnp.abs(pos - n) == lag).astype(F32).astype(BF16)
        line = jnp.dot(taps_ref[...].astype(BF16), spread, preferred_element_type=F32)
        t = lax.broadcasted_iota(jnp.int32, (n, n), 0)
        s = lax.broadcasted_iota(jnp.int32, (n, n), 1)
        distance = jnp.abs(t - s)
        for a in range(arcs):
            wide = jnp.broadcast_to(line[a:a + 1], (n, 2 * n))
            rolled = pltpu.roll(wide, 0, 1, stride=1, stride_axis=0)[:, n:]
            o_ref[a] = jnp.where(distance < band_ref[a], rolled, 0.0).astype(BF16)

    return pl.pallas_call(
        kernel,
        grid_spec=pltpu.PrefetchScalarGridSpec(
            num_scalar_prefetch=1, grid=(1,),
            in_specs=[pl.BlockSpec((arcs, n), lambda i, b: (0, 0))],
            out_specs=pl.BlockSpec((arcs, n, n), lambda i, b: (0, 0, 0))),
        out_shape=sds((arcs, n, n)), name="build_filters")(band, taps)


def pick_pieces(index, mine, other):
    count = mine.shape[0]

    def kernel(i_ref, m_ref, t_ref, o_ref):
        for i in range(count):
            at = i_ref[i]

            @pl.when(at < count)
            def _():
                o_ref[i] = m_ref[at]

            @pl.when(at >= count)
            def _():
                o_ref[i] = t_ref[at - count]

    whole = pl.BlockSpec(mine.shape, lambda i, s: (0, 0, 0))
    return pl.pallas_call(
        kernel,
        grid_spec=pltpu.PrefetchScalarGridSpec(
            num_scalar_prefetch=1, grid=(1,), in_specs=[whole, whole], out_specs=whole),
        out_shape=sds(mine.shape), name="pick_pieces")(index, mine, other)


def filter_piece(arc, filters, piece):
    n, width = piece.shape

    def kernel(a_ref, f_ref, p_ref, o_ref):
        o_ref[...] = jnp.dot(f_ref[0], p_ref[...], preferred_element_type=F32).astype(BF16)

    return pl.pallas_call(
        kernel,
        grid_spec=pltpu.PrefetchScalarGridSpec(
            num_scalar_prefetch=1, grid=(1,),
            in_specs=[pl.BlockSpec((1, n, n), lambda i, a: (a[0], 0, 0)),
                      pl.BlockSpec((n, width), lambda i, a: (0, 0))],
            out_specs=pl.BlockSpec((n, width), lambda i, a: (0, 0))),
        out_shape=sds((n, width)), name="filter_piece")(arc, filters, piece)


def filter_own(places, filters, shards):
    arcs, n, _ = filters.shape
    _, _, part, width = shards[0].shape
    count = len(shards)

    def kernel(p_ref, f_ref, *refs):
        shard_refs, o_ref, line = refs[:count], refs[count], refs[count + 1]
        for i in range(count):
            line[pl.ds(pl.multiple_of(p_ref[i] * part, part), part), :] = shard_refs[i][0, 0]
        o_ref[0] = lax.dot_general(
            line[...], f_ref[0], (((0,), (0,)), ((), ())), preferred_element_type=F32).astype(BF16)

    return pl.pallas_call(
        kernel,
        grid_spec=pltpu.PrefetchScalarGridSpec(
            num_scalar_prefetch=1, grid=(arcs, Z),
            in_specs=[pl.BlockSpec((1, n, n), lambda a, q, p: (a, 0, 0))]
            + [pl.BlockSpec((1, 1, part, width), lambda a, q, p: (q, a, 0, 0))] * count,
            out_specs=pl.BlockSpec((1, width, n), lambda a, q, p: (a, q, 0)),
            scratch_shapes=[pltpu.VMEM((n, width), BF16)]),
        out_shape=sds((arcs, Z * width, n)), name="filter_own")(places, filters, *shards)


def multiply(arcs_at, columns, own, pieces, out, scale, out_shape, tile):
    _, rows, n = own.shape
    width = pieces[0][0][0].shape[1]
    flat = [piece for strip in pieces for slot in strip for piece in slot]
    per_strip = len(flat) // 2

    def kernel(a_ref, c_ref, own_ref, *refs):
        piece_refs, o_ref = refs[:len(flat)], refs[-1]

        for strip in range(2):
            @pl.when(pl.program_id(1) == strip)
            def _():
                total = None
                at = strip * per_strip
                for slot in range(2):
                    start = 0
                    for _piece in pieces[strip][slot]:
                        size = _piece.shape[0]
                        part = jnp.dot(own_ref[a_ref[slot], :, start:start + size],
                                       piece_refs[at][...], preferred_element_type=F32)
                        total = part if total is None else total + part
                        start += size
                        at += 1
                o_ref[...] = total * scale

    specs = [pl.BlockSpec((2, tile, n), lambda m, s, a, c: (0, m, 0))]
    specs += [pl.BlockSpec(piece.shape, lambda m, s, a, c: (0, 0)) for piece in flat]
    operands = [own, *flat]
    aliases = {}
    if out is not None:
        specs.append(pl.BlockSpec(memory_space=pl.ANY))
        operands.append(out)
        aliases = {2 + len(operands) - 1: 0}
    return pl.pallas_call(
        kernel,
        grid_spec=pltpu.PrefetchScalarGridSpec(
            num_scalar_prefetch=2, grid=(rows // tile, 2), in_specs=specs,
            out_specs=pl.BlockSpec((tile, width), lambda m, s, a, c: (m, c[s]))),
        out_shape=out_shape, input_output_aliases=aliases, name="multiply")(arcs_at, columns, *operands)


def per_device(design, filter_taps, band_limit, col_order):
    cols = design.shape[1]
    arcs, n = filter_taps.shape
    x, yl = lax.axis_index("x"), lax.axis_index("yl")
    z, yh, c = lax.axis_index("z"), lax.axis_index("yh"), lax.axis_index("c")
    half, width = design.shape[0] // 2, cols // Z

    shard = split_shard(design)

    shard_y = shift(shard, "yl", YL)
    shards, places = [], []
    for base, row in ((shard, yl), (shard_y, 1 - yl)):
        for step in (0, 1, -1, 2):
            shards.append(shift(base, "x", X, step) if step else base)
            places.append(((x - step) % X) * YL + row)
    filters = build_filters(filter_taps, band_limit)

    mine = lax.all_to_all(shard.reshape(Z * YH, half, width), ("z", "yh"), 0, 0, tiled=True)
    other = shift(mine, "c", C)
    block = col_order.reshape(X * YL, C)[:, c]
    index = block // C + jnp.where(block % C == c, 0, Z * YH)
    picked = pick_pieces(index.astype(jnp.int32), mine, other)
    raw = lax.all_to_all(picked, ("x", "yl"), 0, 0, tiled=True).reshape(n, width)
    g = filter_piece(yh.astype(jnp.int32)[None], filters, raw)

    gy = shift(g, "yh", YH)
    near = {0: (g, gy)}
    for step in (1, -1):
        near[step] = (shift(g, "z", Z, step), shift(gy, "z", Z, step))
    far = []
    for slot in range(2):
        low = shift(near[1][slot][: n // 2], "z", Z, 1)
        high = shift(near[-1][slot][n // 2:], "z", Z, -1)
        far.append([low, high])

    own = filter_own(jnp.stack(places).astype(jnp.int32), filters, shards)
    arcs_at = jnp.stack([yh, 1 - yh]).astype(jnp.int32)
    out_shape = sds((cols, C * cols), F32)
    scale = 1.0 / (arcs * n)
    out = None
    for step, pair in ((0, [[g], [gy]]), (1, [[t] for t in near[1]]), (-1, [[t] for t in near[-1]]), (2, far)):
        crossed = [[shift(t, "c", C) for t in slot] for slot in pair]
        quarter = (z - step) % Z
        columns = jnp.stack([c * Z + quarter, (1 - c) * Z + quarter]).astype(jnp.int32)
        out = multiply(arcs_at, columns, own, [pair, crossed], out, scale, out_shape, cols // 3)
    return out


def solution(mesh):
    torus = Mesh(mesh.devices.reshape(X, YL, Z, YH, C), ("x", "yl", "z", "yh", "c"))
    obs, par = ("x", "yl"), ("z", "yh", "c")
    return jax.shard_map(
        per_device, mesh=torus, in_specs=(P(obs, par), P(), P(), P()), out_specs=P(par, obs), check_vma=False
    )
```

```python
import jax
import jax.numpy as jnp
from jax import lax
from jax.experimental import pallas as pl
from jax.experimental.pallas import tpu as pltpu
from jax.sharding import Mesh
from jax.sharding import PartitionSpec as P


X, YL, Z, YH, C = 4, 2, 4, 2, 2
BF16 = jnp.bfloat16
F32 = jnp.float32
VMEM = pl.BlockSpec(memory_space=pltpu.VMEM)
SMEM = pl.BlockSpec(memory_space=pltpu.SMEM)
ANY = pl.BlockSpec(memory_space=pl.ANY)


def shift(array, axis, size, step=1):
    return lax.ppermute(array, axis, [(i, (i + step) % size) for i in range(size)])


def sds(shape, dtype=BF16):
    return jax.ShapeDtypeStruct(shape, dtype)


def near(array):
    return pltpu.with_memory_space_constraint(array, pltpu.VMEM)


def limit(mib):
    return pltpu.CompilerParams(vmem_limit_bytes=mib << 20)


def split_shard(design):
    rows, cols = design.shape
    half, width = rows // 2, cols // Z

    def kernel(d_ref, o_ref):
        r = lax.broadcasted_iota(jnp.int32, (rows, rows), 0)
        s = lax.broadcasted_iota(jnp.int32, (rows, rows), 1)
        source = jnp.where(r < half, 2 * r, 2 * (r - half) + 1)
        pick = (s == source).astype(F32).astype(BF16)
        sorted_rows = jnp.dot(pick, d_ref[...], preferred_element_type=F32).astype(BF16)
        for q in range(Z):
            for a in range(2):
                o_ref[q, a] = sorted_rows[a * half:(a + 1) * half, q * width:(q + 1) * width]

    return pl.pallas_call(kernel, out_shape=sds((Z, 2, half, width)), in_specs=[VMEM], out_specs=VMEM,
                          compiler_params=limit(4), name="split_shard")(design)


def build_filters(taps, band):
    arcs, n = taps.shape

    def kernel(band_ref, taps_ref, o_ref):
        lag = lax.broadcasted_iota(jnp.int32, (n, 2 * n), 0)
        pos = lax.broadcasted_iota(jnp.int32, (n, 2 * n), 1)
        spread = (jnp.abs(pos - n) == lag).astype(F32).astype(BF16)
        line = jnp.dot(taps_ref[...].astype(BF16), spread, preferred_element_type=F32)
        t = lax.broadcasted_iota(jnp.int32, (n, n), 0)
        s = lax.broadcasted_iota(jnp.int32, (n, n), 1)
        distance = jnp.abs(t - s)
        for a in range(arcs):
            wide = jnp.broadcast_to(line[a:a + 1], (n, 2 * n))
            rolled = pltpu.roll(wide, 0, 1, stride=1, stride_axis=0)[:, n:]
            o_ref[a] = jnp.where(distance < band_ref[a], rolled, 0.0).astype(BF16)

    return pl.pallas_call(kernel, out_shape=sds((arcs, n, n)), in_specs=[SMEM, VMEM], out_specs=VMEM,
                          compiler_params=limit(16), name="build_filters")(band, taps)


def pick_pieces(order, mine, other):
    count = mine.shape[0]

    def kernel(order_ref, mine_ref, other_ref, o_ref):
        core = lax.axis_index("c")
        for i in range(count):
            block = order_ref[i * C + core]
            here = lax.rem(block, C) == core

            @pl.when(here)
            def _():
                o_ref[i] = mine_ref[block // C]

            @pl.when(jnp.logical_not(here))
            def _():
                o_ref[i] = other_ref[block // C]

    return pl.pallas_call(kernel, out_shape=sds(mine.shape), in_specs=[SMEM, VMEM, VMEM], out_specs=VMEM,
                          compiler_params=limit(4), name="pick_pieces")(order, near(mine), near(other))


def filter_piece(filters, piece):
    def kernel(f_ref, p_ref, o_ref):
        o_ref[...] = jnp.dot(f_ref[lax.axis_index("yh")], p_ref[...], preferred_element_type=F32).astype(BF16)

    return pl.pallas_call(kernel, out_shape=sds(piece.shape), in_specs=[VMEM, VMEM], out_specs=VMEM,
                          compiler_params=limit(8), name="filter_piece")(near(filters), near(piece))


def filter_own(filters, pieces):
    arcs, n, _ = filters.shape
    _, _, part, width = pieces[0][0].shape
    count = len(pieces)

    def kernel(f_ref, *refs):
        o_ref, line = refs[count], refs[count + 1]
        x, yl = lax.axis_index("x"), lax.axis_index("yl")
        for a in range(arcs):
            for ref, (array, first, x_step, y_step) in zip(refs, pieces):
                place = lax.rem(x - x_step + X, X) * YL + (1 - yl if y_step else yl)
                rows = pl.ds(pl.multiple_of(place * part, part), part)
                for q in range(array.shape[0]):
                    line[a, rows, (first + q) * width:(first + q + 1) * width] = ref[q, a]
            o_ref[:, a * n:(a + 1) * n] = lax.dot_general(
                line[a], f_ref[a], (((0,), (0,)), ((), ())), preferred_element_type=F32).astype(BF16)

    return pl.pallas_call(
        kernel, out_shape=sds((Z * width, arcs * n)), in_specs=[VMEM] * (1 + count), out_specs=VMEM,
        scratch_shapes=[pltpu.VMEM((arcs, n, Z * width), BF16)],
        compiler_params=limit(20), name="filter_own")(near(filters), *[near(p[0]) for p in pieces])


def multiply(own, chunks, out, scale, out_shape, tile):
    rows, depth = own.shape
    n = depth // 2
    width = chunks[0][1][0][0][0].shape[1]
    flat = [piece for _, pair in chunks for slots in pair for slot in slots for piece in slot]
    jobs = [(m, j) for j in range(len(chunks)) for m in range(rows // tile)]
    slots_out = min(len(jobs), 6)

    def kernel(own_ref, *refs):
        piece_refs, (o_ref, buf, sem, line) = iter(refs[:len(flat)]), refs[-4:]
        yh, core, z = lax.axis_index("yh"), lax.axis_index("c"), lax.axis_index("z")
        for j, (_, pair) in enumerate(chunks):
            for i, slots in enumerate(pair):
                for k, pieces in enumerate(slots):
                    start = (1 - yh if k else yh) * n
                    for piece in pieces:
                        at = pl.ds(pl.multiple_of(start, n // 2), piece.shape[0])
                        line[j, at, i * width:(i + 1) * width] = next(piece_refs)[...]
                        start += piece.shape[0]
        copies = []
        for i, (m, j) in enumerate(jobs):
            if i >= slots_out:
                for copy in copies[i - slots_out]:
                    copy.wait()
            block = pl.ds(m * tile, tile)
            slot = i % slots_out
            product = jnp.dot(own_ref[block, :], line[j], preferred_element_type=F32) * scale
            copies.append([])
            for k in range(2):
                buf[slot, k] = product[:, k * width:(k + 1) * width]
                column = (1 - core if k else core) * Z + lax.rem(z - chunks[j][0] + Z, Z)
                copy = pltpu.make_async_copy(
                    buf.at[slot, k], o_ref.at[block, pl.ds(pl.multiple_of(column * width, width), width)],
                    sem.at[slot, k])
                copy.start()
                copies[-1].append(copy)
        for pair in copies[-slots_out:]:
            for copy in pair:
                copy.wait()

    operands = [near(t) for t in (own, *flat)]
    specs = [VMEM] * len(operands)
    aliases = {}
    if out is not None:
        aliases = {len(operands): 0}
        operands.append(out)
        specs.append(ANY)
    return pl.pallas_call(
        kernel, out_shape=out_shape, in_specs=specs, out_specs=ANY, input_output_aliases=aliases,
        scratch_shapes=[pltpu.VMEM((slots_out, 2, tile, width), F32), pltpu.SemaphoreType.DMA((slots_out, 2)),
                        pltpu.VMEM((len(chunks), depth, 2 * width), BF16)],
        compiler_params=limit(24))(*operands)


def per_device(design, filter_taps, band_limit, col_order):
    cols = design.shape[1]
    arcs, n = filter_taps.shape
    half, width = design.shape[0] // 2, cols // Z

    shard = split_shard(design)
    mine = lax.all_to_all(shard.reshape(Z * YH, half, width), ("z", "yh"), 0, 0, tiled=True)
    filters = build_filters(filter_taps, band_limit)

    shard_y = shift(shard, "yl", YL)
    up = shift(shard, "x", X, 1)
    down = shift(shard, "x", X, -1)
    up_y = shift(shard_y, "x", X, 1)
    down_y = shift(shard_y, "x", X, -1)
    far = shift(up, "x", X, 1)
    far_y = shift(down_y, "x", X, -1)
    own_pieces = [(shard, 0, 0, 0), (up, 0, 1, 0), (down, 0, -1, 0), (far, 0, 2, 0),
                  (shard_y, 0, 0, 1), (up_y, 0, 1, 1), (down_y, 0, -1, 1), (far_y, 0, 2, 1)]

    other = shift(mine, "c", C)
    picked = pick_pieces(col_order, mine, other)
    raw = lax.all_to_all(picked, ("x", "yl"), 0, 0, tiled=True).reshape(n, width)
    g = filter_piece(filters, raw)

    gy = shift(g, "yh", YH)
    up = shift(g, "z", Z, 1)
    down = shift(g, "z", Z, -1)
    up_y = shift(gy, "z", Z, 1)
    down_y = shift(down, "yh", YH)
    far = shift(down, "z", Z, -1)
    far_y = [shift(up_y[: n // 2], "z", Z, 1), shift(far[n // 2:], "yh", YH)]

    own = filter_own(filters, own_pieces)
    out_shape = sds((cols, C * cols), F32)
    scale = 1.0 / (arcs * n)
    chunks = []
    for step, pair in ((0, [[g], [gy]]), (1, [[up], [up_y]]), (-1, [[down], [down_y]]), (2, [[far], far_y])):
        crossed = [[shift(t, "c", C) for t in slot] for slot in pair]
        chunks.append((step, [pair, crossed]))
    out = multiply(own, chunks[:3], None, scale, out_shape, cols // 6)
    return multiply(own, chunks[3:], out, scale, out_shape, cols // 6)


def solution(mesh):
    torus = Mesh(mesh.devices.reshape(X, YL, Z, YH, C), ("x", "yl", "z", "yh", "c"))
    obs, par = ("x", "yl"), ("z", "yh", "c")

    return jax.shard_map(
        per_device, mesh=torus, in_specs=(P(obs, par), P(), P(), P()), out_specs=P(par, obs), check_vma=False
    )
```

```python
import jax
import jax.numpy as jnp
from jax import lax
from jax.experimental import pallas as pl
from jax.experimental.pallas import tpu as pltpu
from jax.sharding import Mesh
from jax.sharding import PartitionSpec as P


X, YL, Z, YH, C = 4, 2, 4, 2, 2
BF16 = jnp.bfloat16
F32 = jnp.float32
VMEM = pl.BlockSpec(memory_space=pltpu.VMEM)
SMEM = pl.BlockSpec(memory_space=pltpu.SMEM)
ANY = pl.BlockSpec(memory_space=pl.ANY)
HBM = pl.BlockSpec(memory_space=pltpu.HBM)


def shift(array, axis, size, step=1):
    return lax.ppermute(array, axis, [(i, (i + step) % size) for i in range(size)])


def sds(shape, dtype=BF16):
    return jax.ShapeDtypeStruct(shape, dtype)


def near(array):
    return pltpu.with_memory_space_constraint(array, pltpu.VMEM)


def limit(mib):
    return pltpu.CompilerParams(vmem_limit_bytes=mib << 20)


def split_shard(design, order):
    rows, cols = design.shape
    half, width = rows // 2, cols // Z

    def kernel(d_ref, order_ref, o_ref, staged_ref, wide, split, sem):
        stage = pltpu.make_async_copy(order_ref, staged_ref, sem.at[2 * Z])
        reads = [pltpu.make_async_copy(d_ref.at[:, pl.ds(q * width, width)], wide.at[q], sem.at[q]) for q in range(Z)]
        writes = [pltpu.make_async_copy(split.at[q], o_ref.at[q], sem.at[Z + q]) for q in range(Z)]
        for read in reads:
            read.start()
        stage.start()
        r = lax.broadcasted_iota(jnp.int32, (rows, rows), 0)
        s = lax.broadcasted_iota(jnp.int32, (rows, rows), 1)
        source = jnp.where(r < half, 2 * r, 2 * (r - half) + 1)
        pick = (s == source).astype(F32).astype(BF16)
        for q in range(Z):
            reads[q].wait()
            sorted_rows = jnp.dot(pick, wide[q], preferred_element_type=F32).astype(BF16)
            for a in range(2):
                split[q, a] = sorted_rows[a * half:(a + 1) * half, :]
            writes[q].start()
        for write in writes:
            write.wait()
        stage.wait()

    far = lambda array: pltpu.with_memory_space_constraint(array, pltpu.HBM)
    return pl.pallas_call(kernel, out_shape=(sds((Z, 2, half, width)), sds(order.shape, jnp.int32)),
                          in_specs=[HBM, HBM], out_specs=(ANY, VMEM),
                          scratch_shapes=[pltpu.VMEM((Z, rows, width), BF16), pltpu.VMEM((Z, 2, half, width), BF16),
                                          pltpu.SemaphoreType.DMA((2 * Z + 1,))],
                          compiler_params=limit(4), name="split_shard")(far(design), far(order))


def build_filters(taps, band):
    arcs, n = taps.shape

    def kernel(band_ref, taps_ref, o_ref):
        lag = lax.broadcasted_iota(jnp.int32, (n, 2 * n), 0)
        pos = lax.broadcasted_iota(jnp.int32, (n, 2 * n), 1)
        spread = (jnp.abs(pos - n) == lag).astype(F32).astype(BF16)
        line = jnp.dot(taps_ref[...].astype(BF16), spread, preferred_element_type=F32)
        t = lax.broadcasted_iota(jnp.int32, (n, n), 0)
        s = lax.broadcasted_iota(jnp.int32, (n, n), 1)
        distance = jnp.abs(t - s)
        for a in range(arcs):
            wide = jnp.broadcast_to(line[a:a + 1], (n, 2 * n))
            rolled = pltpu.roll(wide, 0, 1, stride=1, stride_axis=0)[:, n:]
            o_ref[a] = jnp.where(distance < band_ref[a], rolled, 0.0).astype(BF16)

    return pl.pallas_call(kernel, out_shape=sds((arcs, n, n)), in_specs=[SMEM, VMEM], out_specs=VMEM,
                          compiler_params=limit(16), name="build_filters")(band, taps)


def pick_pieces(order, mine, other):
    count = mine.shape[0]

    def kernel(order_ref, mine_ref, other_ref, o_ref, sem):
        core = lax.axis_index("c")
        for i in range(count):
            block = order_ref[i * C + core]
            here = lax.rem(block, C) == core

            @pl.when(here)
            def _():
                pltpu.make_async_copy(mine_ref.at[block // C], o_ref.at[i], sem.at[i]).start()

            @pl.when(jnp.logical_not(here))
            def _():
                pltpu.make_async_copy(other_ref.at[block // C], o_ref.at[i], sem.at[i]).start()

        for i in range(count):
            pltpu.make_async_copy(mine_ref.at[0], o_ref.at[i], sem.at[i]).wait()

    return pl.pallas_call(kernel, out_shape=sds(mine.shape), in_specs=[SMEM, VMEM, VMEM], out_specs=ANY,
                          scratch_shapes=[pltpu.SemaphoreType.DMA((count,))],
                          compiler_params=limit(4), name="pick_pieces")(near(order), near(mine), near(other))


def filter_piece(filters, piece):
    def kernel(f_ref, p_ref, o_ref):
        o_ref[...] = jnp.dot(f_ref[lax.axis_index("yh")], p_ref[...], preferred_element_type=F32).astype(BF16)

    return pl.pallas_call(kernel, out_shape=sds(piece.shape), in_specs=[VMEM, VMEM], out_specs=VMEM,
                          compiler_params=limit(8), name="filter_piece")(near(filters), near(piece))


def filter_own(filters, pieces):
    arcs, n, _ = filters.shape
    _, _, part, width = pieces[0][0].shape
    count = len(pieces)

    def kernel(f_ref, *refs):
        o_ref, line = refs[count], refs[count + 1]
        x, yl = lax.axis_index("x"), lax.axis_index("yl")
        for a in range(arcs):
            for ref, (array, first, x_step, y_step) in zip(refs, pieces):
                place = lax.rem(x - x_step + X, X) * YL + (1 - yl if y_step else yl)
                rows = pl.ds(pl.multiple_of(place * part, part), part)
                for q in range(array.shape[0]):
                    line[a, rows, (first + q) * width:(first + q + 1) * width] = ref[q, a]
            o_ref[:, a * n:(a + 1) * n] = lax.dot_general(
                line[a], f_ref[a], (((0,), (0,)), ((), ())), preferred_element_type=F32).astype(BF16)

    return pl.pallas_call(
        kernel, out_shape=sds((Z * width, arcs * n)), in_specs=[VMEM] * (1 + count), out_specs=VMEM,
        scratch_shapes=[pltpu.VMEM((arcs, n, Z * width), BF16)],
        compiler_params=limit(20), name="filter_own")(near(filters), *[near(p[0]) for p in pieces])


def multiply(own, chunks, out, scale, out_shape, tile):
    rows, depth = own.shape
    n = depth // 2
    width = chunks[0][1][0][0][0].shape[1]
    flat = [piece for _, pair in chunks for slots in pair for slot in slots for piece in slot]
    jobs = [(m, j) for j in range(len(chunks)) for m in range(rows // tile)]
    slots_out = min(len(jobs), 18)

    def kernel(own_ref, *refs):
        piece_refs, (o_ref, buf, sem, line) = iter(refs[:len(flat)]), refs[-4:]
        yh, core, z = lax.axis_index("yh"), lax.axis_index("c"), lax.axis_index("z")
        for j, (_, pair) in enumerate(chunks):
            for i, slots in enumerate(pair):
                for k, pieces in enumerate(slots):
                    start = (1 - yh if k else yh) * n
                    for piece in pieces:
                        at = pl.ds(pl.multiple_of(start, n // 2), piece.shape[0])
                        line[j, at, i * width:(i + 1) * width] = next(piece_refs)[...]
                        start += piece.shape[0]
        copies = []
        for i, (m, j) in enumerate(jobs):
            if i >= slots_out:
                for copy in copies[i - slots_out]:
                    copy.wait()
            block = pl.ds(m * tile, tile)
            slot = i % slots_out
            product = jnp.dot(own_ref[block, :], line[j], preferred_element_type=F32) * scale
            copies.append([])
            for k in range(2):
                buf[slot, k] = product[:, k * width:(k + 1) * width]
                column = (1 - core if k else core) * Z + lax.rem(z - chunks[j][0] + Z, Z)
                copy = pltpu.make_async_copy(
                    buf.at[slot, k], o_ref.at[block, pl.ds(pl.multiple_of(column * width, width), width)],
                    sem.at[slot, k])
                copy.start()
                copies[-1].append(copy)
        for pair in copies[-slots_out:]:
            for copy in pair:
                copy.wait()

    operands = [near(t) for t in (own, *flat)]
    specs = [VMEM] * len(operands)
    aliases = {}
    if out is not None:
        aliases = {len(operands): 0}
        operands.append(out)
        specs.append(ANY)
    return pl.pallas_call(
        kernel, out_shape=out_shape, in_specs=specs, out_specs=ANY, input_output_aliases=aliases,
        scratch_shapes=[pltpu.VMEM((slots_out, 2, tile, width), F32), pltpu.SemaphoreType.DMA((slots_out, 2)),
                        pltpu.VMEM((len(chunks), depth, 2 * width), BF16)],
        compiler_params=limit(36))(*operands)


def per_device(design, filter_taps, band_limit, col_order):
    cols = design.shape[1]
    arcs, n = filter_taps.shape
    half, width = design.shape[0] // 2, cols // Z

    shard, order = split_shard(design, col_order)
    mine = lax.all_to_all(shard.reshape(Z * YH, half, width), ("z", "yh"), 0, 0, tiled=True)
    filters = build_filters(filter_taps, band_limit)

    shard_y = shift(shard, "yl", YL)
    up = shift(shard, "x", X, 1)
    down = shift(shard, "x", X, -1)
    up_y = shift(shard_y, "x", X, 1)
    down_y = shift(shard_y, "x", X, -1)
    far = shift(up, "x", X, 1)
    far_y = shift(down_y, "x", X, -1)
    own_pieces = [(shard, 0, 0, 0), (up, 0, 1, 0), (down, 0, -1, 0), (far, 0, 2, 0),
                  (shard_y, 0, 0, 1), (up_y, 0, 1, 1), (down_y, 0, -1, 1), (far_y, 0, 2, 1)]

    other = shift(mine, "c", C)
    picked = pick_pieces(order, mine, other)
    raw = lax.all_to_all(picked, ("x", "yl"), 0, 0, tiled=True).reshape(n, width)
    g = filter_piece(filters, raw)

    gy = shift(g, "yh", YH)
    up = shift(g, "z", Z, 1)
    down = shift(g, "z", Z, -1)
    up_y = shift(gy, "z", Z, 1)
    down_y = shift(down, "yh", YH)
    far = shift(down, "z", Z, -1)
    far_y = [shift(up_y, "z", Z, 1)]

    own = filter_own(filters, own_pieces)
    out_shape = sds((cols, C * cols), F32)
    scale = 1.0 / (arcs * n)
    chunks = []
    for step, pair in ((0, [[g], [gy]]), (1, [[up], [up_y]]), (-1, [[down], [down_y]]), (2, [[far], far_y])):
        crossed = [[shift(t, "c", C) for t in slot] for slot in pair]
        chunks.append((step, [pair, crossed]))
    out = None
    for part in (chunks[:1], chunks[1:3], chunks[3:]):
        out = multiply(own, part, out, scale, out_shape, cols // 6)
    return out


def solution(mesh):
    torus = Mesh(mesh.devices.reshape(X, YL, Z, YH, C), ("x", "yl", "z", "yh", "c"))
    obs, par = ("x", "yl"), ("z", "yh", "c")

    return jax.shard_map(
        per_device, mesh=torus, in_specs=(P(obs, par), P(), P(), P()), out_specs=P(par, obs), check_vma=False
    )
```
